32 devices in a mesh: wide: 4 (over z), step: 2 (over x), img: 4 (over y, core).
Axes of the slice: x: 2, y: 2, z: 4, core: 2. Of those that a mesh axis runs over, the one named last changes fastest.
Arguments:
- activations: bfloat16 [2, 8, 4096, 2560], P('step', 'img', 'wide'), may hold values from -6 to 6
- cotangents: bfloat16 [2, 8, 4096, 10240], P('step', 'img', 'wide'), may hold values from -6 to 6
- projection: bfloat16 [2560, 512], P('wide'), may hold values from -0.125 to 0.125
- buckets: int32 [10240], replicated, may hold values from 0 to 63
- sign_bits: int32 [10240], replicated, may hold values from 0 to 1
- timesteps: int32 [2, 8], P('step', 'img'), may hold values from 0 to 999
Outputs:
- sketch: float32 [8, 32768], P('img', ('wide', 'step'))
The draws below stay inside these ranges and needn't reach their ends.
Inputs may be any that keep to these rules, and one draw needn't show every extreme that they name: `buckets`: every hidden unit has one bucket.
All inputs are finite; a program needn't handle non-finite values.
Results may differ from the reference program's by a relative error of at most 0.003.
Values may be sent and summed in bfloat16 or wider, within the bound.
No kernel may reach another device: no remote copies, remote signals or barrier semaphores. Data moves between devices by JAX's collectives and lax.ppermute only.
A program may use at most 320 MiB of HBM per device.

```python
import jax
import jax.numpy as jnp
from jax import lax

D = 2560
FF = 10240
PATCHES = 4096
RW = 512
KB = 64
DIFF_STEPS = 1000
IMAGES = 8
STEPS = 2


def touch_ends(result, key, low, top_value):
    longest = result.shape.index(max(result.shape))
    spots = []
    for shift in (0, 1):
        where = [jax.random.randint(jax.random.fold_in(key, axis), (), 0, length) for axis, length in enumerate(result.shape)]
        where[longest] = (where[longest] + shift) % result.shape[longest]
        spots.append(tuple(where))
    return result.at[spots[0]].set(low).at[spots[1]].set(top_value)


def block_scale(own_key, extent, pieces, least, largest):
    factor_of = 1.0
    for axis_at, blocks in pieces:
        steps = jax.random.uniform(jax.random.fold_in(jax.random.fold_in(own_key, 6), axis_at), (blocks,), jnp.float32, least / len(pieces), largest / len(pieces))
        factor_of = factor_of * jnp.repeat(jnp.exp(steps), extent[axis_at] // blocks).reshape((-1,) + (1,) * (len(extent) - 1 - axis_at))
    return factor_of


def scatter_about(stream_key, extent, spread, most, pieces=(), held_as=jnp.bfloat16):
    values = spread * jax.random.normal(stream_key, extent, jnp.float32)
    if pieces:
        values = values * block_scale(stream_key, extent, pieces, -0.22, 0.18)
    return jnp.clip(values, -most, most).astype(held_as)


def setup_inputs(seed: int = 0) -> dict:
    streams_of = jax.random.split(jax.random.key(seed), 7)
    return {
        "activations": scatter_about(streams_of[0], (STEPS, IMAGES, PATCHES, D), 1.0, 6.0, ((0, 2), (1, 4), (2, 4))),
        "cotangents": scatter_about(streams_of[1], (STEPS, IMAGES, PATCHES, FF), 1.0, 6.0, ((0, 2), (1, 4), (2, 4))),
        "projection": scatter_about(streams_of[2], (D, RW), D ** -0.5, 0.125, ((0, 4),)),
        "buckets": touch_ends(jax.random.randint(streams_of[3], (FF,), 0, KB), jax.random.fold_in(streams_of[3], 1), 0, KB - 1).astype(jnp.int32),
        "sign_bits": touch_ends(jax.random.randint(streams_of[4], (FF,), 0, 2), jax.random.fold_in(streams_of[4], 1), 0, 1).astype(jnp.int32),
        "timesteps": touch_ends(jax.random.randint(streams_of[5], (STEPS, IMAGES), 0, DIFF_STEPS), jax.random.fold_in(streams_of[5], 1), 0, DIFF_STEPS - 1).astype(jnp.int32),
    }


def reference(activations, cotangents, projection, buckets, sign_bits, timesteps):
    sign_vals = (2 * sign_bits - 1).astype(jnp.float32)
    weight = 2.0 - 1.5 * timesteps.astype(jnp.float32) / DIFF_STEPS
    act_flat = activations.reshape(STEPS * IMAGES, PATCHES, D)
    cot_flat = cotangents.reshape(STEPS * IMAGES, PATCHES, FF)
    weight_flat = weight.reshape(STEPS * IMAGES)

    def per_image(packed):
        act_rows, cot_rows, weight_one = packed
        projected = jnp.dot(act_rows, projection, preferred_element_type=jnp.float32).astype(jnp.bfloat16)
        grad = jnp.dot(cot_rows.T, projected, preferred_element_type=jnp.float32)
        unit = grad * lax.rsqrt(lax.optimization_barrier(jnp.sum(grad * grad, axis=1, keepdims=True)) + 1e-06)
        bucketed = jax.ops.segment_sum(unit * sign_vals[:, None], buckets, num_segments=KB)
        return (bucketed * weight_one).reshape(KB * RW)
    terms = lax.map(per_image, (act_flat, cot_flat, weight_flat))
    return lax.optimization_barrier(jnp.sum(terms.reshape(STEPS, IMAGES, KB * RW), axis=0))
```

```python
import functools

import jax
import jax.numpy as jnp
import numpy as np
from jax import lax
from jax.experimental import pallas as pl
from jax.experimental.pallas import tpu as pltpu
from jax.sharding import PartitionSpec as P

RW = 512
KB = 64
DIFF_STEPS = 1000
LINE = 4
LAG = 2
HB = 512
FIELDS = 6


def exchange_columns(activations, cotangents, projection, buckets, sign_bits, timesteps):
    image_count = activations.shape[1]
    projected = jnp.einsum(
        "sipd,dr->sipr",
        activations,
        lax.all_gather(projection, "wide", axis=0, tiled=True),
        preferred_element_type=jnp.float32,
    ).astype(jnp.bfloat16)
    weight = 2.0 - 1.5 * timesteps.astype(jnp.float32) / DIFF_STEPS
    sign_vals = (2 * sign_bits - 1).astype(jnp.float32)
    bucket_ids = jnp.arange(KB, dtype=jnp.int32)
    columns = lax.all_to_all(cotangents, "wide", split_axis=3, concat_axis=2, tiled=True)
    col_count = columns.shape[3]
    col_grads = jnp.einsum(
        "sipc,sipr->sicr",
        columns,
        lax.all_gather(projected, "wide", axis=2, tiled=True),
        preferred_element_type=jnp.float32,
    )
    unit = col_grads * lax.rsqrt(jnp.sum(col_grads * col_grads, axis=3, keepdims=True) + 1e-06)
    col_start = lax.axis_index("wide") * col_count
    local_buckets = lax.dynamic_slice_in_dim(buckets, col_start, col_count, 0)
    local_signs = lax.dynamic_slice_in_dim(sign_vals, col_start, col_count, 0)
    bucket_table = jnp.where(
        local_buckets[:, None] == bucket_ids[None, :], local_signs[:, None], 0.0
    )
    sketch_part = jnp.einsum("ck,sicr->sikr", bucket_table, unit, precision=lax.Precision.HIGHEST)
    scaled = sketch_part * weight[:, :, None, None]
    partial_terms = jnp.sum(scaled, axis=0).reshape(image_count, KB * RW)
    return lax.psum_scatter(partial_terms, ("wide", "step"), scatter_dimension=1, tiled=True)


def timetable(units, blocks):
    extras = 2 * LAG
    ups = (units - extras) // 2
    sends = ups + 2 * LAG
    kernels = sends + LAG
    table = np.zeros((LINE, kernels, 2, FIELDS), np.int32)

    def put(z, step, slot, unit, from_left, from_right, send):
        assert not table[z, step, slot, 4:].any()
        table[z, step, slot] = (unit // blocks, unit % blocks, from_left, from_right, send, not send)

    for u in range(ups):
        for hop in range(LINE):
            put(hop, u + hop * LAG, 0, u, hop > 0, False, hop < LINE - 1)
            put(LINE - 1 - hop, u + hop * LAG, 1, ups + u, False, hop > 0, hop < LINE - 1)
    for e in range(LAG):
        to_one, to_two = 2 * ups + e, 2 * ups + LAG + e
        early, late, last = ups + e, ups + LAG + e, ups + 2 * LAG + e
        put(0, early, 0, to_two, False, False, True)
        put(1, late, 0, to_two, True, False, True)
        put(3, late, 1, to_two, False, False, True)
        put(2, last, 1, to_two, True, True, False)
        put(3, early, 1, to_one, False, False, True)
        put(2, late, 1, to_one, False, True, True)
        put(0, late, 0, to_one, False, False, True)
        put(1, last, 0, to_one, True, True, False)
    return table, sends


def project_body(where, act_ref, own_ref, *refs):
    (*parts, out_ref) = refs
    same, other = parts[: LINE - 1], parts[LINE - 1 :]
    depth = own_ref.shape[0]
    half = own_ref.shape[1] // 2
    for side, given in ((0, same), (1, other)):
        at = pl.multiple_of(where[LINE + side] * half, half)
        total = None
        for s in range(LINE):
            w = own_ref[:, pl.ds(at, half)] if s == 0 else given[s - 1][...]
            a = act_ref[0, 0, :, pl.ds(pl.multiple_of(where[s] * depth, depth), depth)]
            term = lax.dot_general(
                w, a, (((0,), (1,)), ((), ())), preferred_element_type=jnp.float32
            )
            total = term if total is None else total + term
        out_ref[0, pl.ds(at, half), :] = total.astype(jnp.bfloat16)


def project(where, activations, own, same, other):
    _, images, patches, width = activations.shape
    part = pl.BlockSpec(same[0].shape, lambda i, w: (0, 0))
    return pl.pallas_call(
        project_body,
        out_shape=jax.ShapeDtypeStruct((images, RW, patches), jnp.bfloat16),
        grid_spec=pltpu.PrefetchScalarGridSpec(
            num_scalar_prefetch=1,
            grid=(images,),
            in_specs=[
                pl.BlockSpec((1, 1, patches, width), lambda i, w: (0, i, 0, 0)),
                pl.BlockSpec(own.shape, lambda i, w: (0, 0)),
            ]
            + [part] * (2 * (LINE - 1)),
            out_specs=pl.BlockSpec((1, RW, patches), lambda i, w: (i, 0, 0)),
        ),
        compiler_params=pltpu.CompilerParams(vmem_limit_bytes=40 << 20),
        cost_estimate=pl.CostEstimate(
            flops=2 * images * patches * width * RW,
            bytes_accessed=2 * images * patches * (width + RW),
            transcendentals=0,
        ),
    )(where, activations, own, *same, *other)


def step_body(step, sends, todo, cot_ref, proj_ref, code_ref, *refs):
    refs = list(refs)
    left_ref, right_ref = (refs.pop(0), refs.pop(0)) if step >= LAG else (None, None)
    sketch_in = refs.pop(0)
    up_ref, down_ref = (refs.pop(0), refs.pop(0)) if step < sends else (None, None)
    sketch_out, total = refs
    slot = pl.program_id(0)
    base = (step * 2 + slot) * FIELDS
    image = todo[base]
    send, finish = todo[base + 4], todo[base + 5]

    @pl.when(slot == 0)
    def _():
        sketch_out[...] = sketch_in[...]

    @pl.when(send + finish > 0)
    def _():
        total[...] = jnp.dot(proj_ref[0], cot_ref[0, 0], preferred_element_type=jnp.float32)

    if left_ref is not None:
        for flag, came in ((2, left_ref), (3, right_ref)):

            @pl.when(todo[base + flag] > 0)
            def _(came=came):
                total[...] += came[...].astype(jnp.float32)

    if up_ref is not None:
        for side, out in enumerate((up_ref, down_ref)):

            @pl.when((slot == side) & (send > 0))
            def _(out=out):
                out[...] = total[...].astype(jnp.bfloat16)

    if step >= LAG:

        @pl.when(finish > 0)
        def _():
            grad = total[...]
            scale = lax.rsqrt(jnp.sum(grad * grad, axis=0, keepdims=True) + 1e-06)
            unit = grad * scale
            high = unit.astype(jnp.bfloat16)
            low = (unit - high.astype(jnp.float32)).astype(jnp.bfloat16)
            code = code_ref[...]
            rows = lax.broadcasted_iota(jnp.int32, (KB, code.shape[1]), 0)
            sign = (2 * (code & 1) - 1).astype(jnp.float32)
            pick = jnp.where(rows == (code >> 1), sign, 0.0).astype(jnp.bfloat16)
            dims = (((1,), (1,)), ((), ()))
            part = lax.dot_general(pick, high, dims, preferred_element_type=jnp.float32)
            part += lax.dot_general(pick, low, dims, preferred_element_type=jnp.float32)
            sketch_out[image] += part


def one_step(step, sends, todo, cotangents, projected, code, came, sketch):
    _, images, patches, _ = cotangents.shape
    block = (RW, HB)

    def fixed(i, t):
        return (0, 0)

    def whole(i, t):
        return (0, 0, 0)

    def at(i, field, t):
        return t[(step * 2 + i) * FIELDS + field]

    moving = step < sends
    piece = pl.BlockSpec(block, fixed)
    total = pl.BlockSpec(sketch.shape, whole)
    out = pl.pallas_call(
        functools.partial(step_body, step, sends),
        out_shape=[jax.ShapeDtypeStruct(block, jnp.bfloat16)] * (2 * moving)
        + [jax.ShapeDtypeStruct(sketch.shape, jnp.float32)],
        grid_spec=pltpu.PrefetchScalarGridSpec(
            num_scalar_prefetch=1,
            grid=(2,),
            in_specs=[
                pl.BlockSpec((1, 1, patches, HB), lambda i, t: (0, at(i, 0, t), 0, at(i, 1, t))),
                pl.BlockSpec((1, RW, patches), lambda i, t: (at(i, 0, t), 0, 0)),
                pl.BlockSpec((1, HB), lambda i, t: (0, at(i, 1, t))),
            ]
            + [piece] * len(came)
            + [total],
            out_specs=[piece] * (2 * moving) + [total],
            scratch_shapes=[pltpu.VMEM(block, jnp.float32)],
        ),
        compiler_params=pltpu.CompilerParams(vmem_limit_bytes=24 << 20),
        cost_estimate=pl.CostEstimate(
            flops=4 * RW * patches * HB,
            bytes_accessed=4 * (RW * patches + HB * patches + 2 * RW * HB),
            transcendentals=0,
        ),
    )(todo, cotangents, projected, code, *came, sketch)
    return out[:-1], out[-1]


def exchange_partials(activations, cotangents, projection, buckets, sign_bits, timesteps):
    images = activations.shape[1]
    hidden = cotangents.shape[3]
    steps = lax.axis_size("step")
    z = lax.axis_index("wide")
    core = lax.axis_index("img") % 2

    half = RW // 2
    mine = lax.dynamic_slice_in_dim(projection, core * half, half, 1)
    pair = [(i, i ^ 1) for i in range(lax.axis_size("img"))]
    same = [
        lax.ppermute(mine, "wide", [(i, (i + s) % LINE) for i in range(LINE)])
        for s in range(1, LINE)
    ]
    other = [lax.ppermute(w, "img", pair) for w in same]
    where = jnp.stack([(z - s) % LINE for s in range(LINE)] + [core, 1 - core]).astype(jnp.int32)
    projected = project(where, activations, projection, same, other)

    blocks = hidden // HB
    table, sends = timetable(images * blocks, blocks)
    todo = lax.dynamic_index_in_dim(jnp.asarray(table.reshape(LINE, -1)), z, 0, keepdims=False)
    code = (2 * buckets + sign_bits).reshape(1, hidden)
    up = [(i, i + 1) for i in range(LINE - 1)]
    down = [(i + 1, i) for i in range(LINE - 1)]
    sketch = jnp.zeros((images, KB, RW), jnp.float32)
    came = []
    for step in range(sends + LAG):
        arrived = came[step - LAG] if step >= LAG else []
        sent, sketch = one_step(step, sends, todo, cotangents, projected, code, arrived, sketch)
        if step < sends:
            came.append([lax.ppermute(sent[0], "wide", up), lax.ppermute(sent[1], "wide", down)])

    weight = 2.0 - 1.5 * timesteps[0].astype(jnp.float32) / DIFF_STEPS
    pieces = LINE * steps
    scaled = (sketch * weight[:, None, None]).reshape(images, pieces, KB // pieces, RW)
    outgoing = jnp.swapaxes(scaled, 0, 1).reshape(pieces, images * (KB // pieces), RW)
    mixed = lax.all_to_all(outgoing, ("wide", "step"), 0, 0, tiled=True)
    return jnp.sum(mixed, axis=0).reshape(images, (KB // pieces) * RW)


def local(activations, cotangents, projection, buckets, sign_bits, timesteps):
    _, images, patches, _ = cotangents.shape
    hidden = cotangents.shape[3]
    pieces = LINE * lax.axis_size("step")
    line = (
        lax.axis_size("wide") == LINE
        and lax.axis_size("img") % 2 == 0
        and patches >= RW
        and hidden % HB == 0
        and (images * (hidden // HB)) % 2 == 0
        and KB % pieces == 0
    )
    plan = exchange_partials if line else exchange_columns
    return plan(activations, cotangents, projection, buckets, sign_bits, timesteps)


def solution(mesh):
    in_specs = (
        P("step", "img", "wide", None),
        P("step", "img", "wide", None),
        P("wide", None),
        P(),
        P(),
        P("step", "img"),
    )
    out_specs = P("img", ("wide", "step"))
    return jax.shard_map(local, mesh=mesh, in_specs=in_specs, out_specs=out_specs, check_vma=False)
```

```python
import functools

import jax
import jax.numpy as jnp
import numpy as np
from jax import lax
from jax.experimental import pallas as pl
from jax.experimental.pallas import tpu as pltpu
from jax.sharding import PartitionSpec as P

RW = 512
KB = 64
DIFF_STEPS = 1000
LINE = 4
LAG = 2
HB = 512
FIELDS = 6
PART = 256
AHEAD = 2


def exchange_columns(activations, cotangents, projection, buckets, sign_bits, timesteps):
    image_count = activations.shape[1]
    projected = jnp.einsum(
        "sipd,dr->sipr",
        activations,
        lax.all_gather(projection, "wide", axis=0, tiled=True),
        preferred_element_type=jnp.float32,
    ).astype(jnp.bfloat16)
    weight = 2.0 - 1.5 * timesteps.astype(jnp.float32) / DIFF_STEPS
    sign_vals = (2 * sign_bits - 1).astype(jnp.float32)
    bucket_ids = jnp.arange(KB, dtype=jnp.int32)
    columns = lax.all_to_all(cotangents, "wide", split_axis=3, concat_axis=2, tiled=True)
    col_count = columns.shape[3]
    col_grads = jnp.einsum(
        "sipc,sipr->sicr",
        columns,
        lax.all_gather(projected, "wide", axis=2, tiled=True),
        preferred_element_type=jnp.float32,
    )
    unit = col_grads * lax.rsqrt(jnp.sum(col_grads * col_grads, axis=3, keepdims=True) + 1e-06)
    col_start = lax.axis_index("wide") * col_count
    local_buckets = lax.dynamic_slice_in_dim(buckets, col_start, col_count, 0)
    local_signs = lax.dynamic_slice_in_dim(sign_vals, col_start, col_count, 0)
    bucket_table = jnp.where(
        local_buckets[:, None] == bucket_ids[None, :], local_signs[:, None], 0.0
    )
    sketch_part = jnp.einsum("ck,sicr->sikr", bucket_table, unit, precision=lax.Precision.HIGHEST)
    scaled = sketch_part * weight[:, :, None, None]
    partial_terms = jnp.sum(scaled, axis=0).reshape(image_count, KB * RW)
    return lax.psum_scatter(partial_terms, ("wide", "step"), scatter_dimension=1, tiled=True)


def timetable(units, blocks):
    extras = 2 * LAG
    ups = (units - extras) // 2
    sends = ups + 2 * LAG
    kernels = sends + LAG
    table = np.zeros((LINE, kernels, 2, FIELDS), np.int32)

    def put(z, step, slot, unit, from_left, from_right, send):
        assert not table[z, step, slot, 4:].any()
        table[z, step, slot] = (unit // blocks, unit % blocks, from_left, from_right, send, not send)

    for u in range(ups):
        for hop in range(LINE):
            put(hop, u + hop * LAG, 0, 2 * u, hop > 0, False, hop < LINE - 1)
            put(LINE - 1 - hop, u + hop * LAG, 1, 2 * u + 1, False, hop > 0, hop < LINE - 1)
    for e in range(LAG):
        to_one, to_two = 2 * ups + e, 2 * ups + LAG + e
        early, late, last = ups + e, ups + LAG + e, ups + 2 * LAG + e
        put(0, early, 0, to_two, False, False, True)
        put(1, late, 0, to_two, True, False, True)
        put(3, late, 1, to_two, False, False, True)
        put(2, last, 1, to_two, True, True, False)
        put(3, early, 1, to_one, False, False, True)
        put(2, late, 1, to_one, False, True, True)
        put(0, late, 0, to_one, False, False, True)
        put(1, last, 0, to_one, True, True, False)
    return table, sends


def project_first_body(where, act_ref, mine_ref, theirs_ref, *refs):
    (*parts, out_ref, proj_ref) = refs
    depth, half = mine_ref.shape

    @pl.when(pl.program_id(0) == 0)
    def _():
        for side, given in ((0, [mine_ref, *parts[: LINE - 1]]), (1, [theirs_ref, *parts[LINE - 1 :]])):
            at = pl.ds(pl.multiple_of(where[LINE + side] * half, half), half)
            for s, piece in enumerate(given):
                rows = pl.ds(pl.multiple_of(where[s] * depth, depth), depth)
                proj_ref[rows, at] = piece[...]

    project_body(act_ref, proj_ref, out_ref)


def project_body(act_ref, proj_ref, out_ref):
    rows = jnp.dot(act_ref[0, 0], proj_ref[...], preferred_element_type=jnp.float32)
    out_ref[0] = rows.astype(jnp.bfloat16).T


def project_later_body(act_ref, proj_ref, held_ref, out_ref):
    project_body(act_ref, proj_ref, out_ref)


def project_cost(patches, width):
    return pl.CostEstimate(
        flops=2 * patches * width * RW,
        bytes_accessed=2 * (patches * (width + RW) + width * RW),
        transcendentals=0,
    )


def project_first(where, activations, pieces):
    _, images, patches, width = activations.shape
    rows = patches // 2
    part = pl.BlockSpec(pieces[0].shape, lambda i, w: (0, 0))
    return pl.pallas_call(
        project_first_body,
        out_shape=[
            jax.ShapeDtypeStruct((images, RW, patches), jnp.bfloat16),
            jax.ShapeDtypeStruct((width, RW), jnp.bfloat16),
        ],
        grid_spec=pltpu.PrefetchScalarGridSpec(
            num_scalar_prefetch=1,
            grid=(2,),
            in_specs=[pl.BlockSpec((1, 1, rows, width), lambda i, w: (0, 0, i, 0))]
            + [part] * len(pieces),
            out_specs=[
                pl.BlockSpec((1, RW, rows), lambda i, w: (0, 0, i)),
                pl.BlockSpec((width, RW), lambda i, w: (0, 0)),
            ],
        ),
        compiler_params=pltpu.CompilerParams(vmem_limit_bytes=44 << 20),
        cost_estimate=project_cost(patches, width),
    )(where, activations, *pieces)


def project_later(image, activations, projection, projected):
    _, images, patches, width = activations.shape
    rows = patches // 2
    return pl.pallas_call(
        project_later_body,
        out_shape=jax.ShapeDtypeStruct(projected.shape, jnp.bfloat16),
        grid=(2,),
        in_specs=[
            pl.BlockSpec((1, 1, rows, width), lambda i: (0, image, i, 0)),
            pl.BlockSpec((width, RW), lambda i: (0, 0)),
            pl.BlockSpec(memory_space=pl.ANY),
        ],
        out_specs=pl.BlockSpec((1, RW, rows), lambda i: (image, 0, i)),
        input_output_aliases={2: 0},
        compiler_params=pltpu.CompilerParams(vmem_limit_bytes=44 << 20),
        cost_estimate=project_cost(patches, width),
    )(activations, projection, projected)


def step_body(step, sends, finishing, todo, cot_ref, code_ref, proj_ref, *refs):
    refs = list(refs)
    left_ref, right_ref = (refs.pop(0), refs.pop(0)) if step >= LAG else (None, None)
    sketch_in = refs.pop(0)
    up_ref, down_ref = (refs.pop(0), refs.pop(0)) if step < sends else (None, None)
    sketch_out, total = refs
    slot = pl.program_id(0)
    base = (step * 2 + slot) * FIELDS
    image = todo[base]
    send, finish = todo[base + 4], todo[base + 5]

    @pl.when(slot == 0)
    def _():
        sketch_out[...] = sketch_in[...]

    @pl.when(send + finish > 0)
    def _():
        total[...] = jnp.dot(proj_ref[0], cot_ref[0, 0], preferred_element_type=jnp.float32)

    if left_ref is not None:
        for flag, came in ((2, left_ref), (3, right_ref)):

            @pl.when(todo[base + flag] > 0)
            def _(came=came):
                total[...] += came[...].astype(jnp.float32)

    if up_ref is not None:
        for side, out in enumerate((up_ref, down_ref)):

            @pl.when((slot == side) & (send > 0))
            def _(out=out):
                out[...] = total[...].astype(jnp.bfloat16)

    if finishing:

        @pl.when(finish > 0)
        def _():
            @pl.loop(0, HB // PART)
            def _(j):
                at = pl.ds(pl.multiple_of(j * PART, PART), PART)
                grad = total[:, at]
                scale = lax.rsqrt(jnp.sum(grad * grad, axis=0, keepdims=True) + 1e-06)
                unit = grad * scale
                high = unit.astype(jnp.bfloat16)
                low = (unit - high.astype(jnp.float32)).astype(jnp.bfloat16)
                code = code_ref[:, at]
                rows = lax.broadcasted_iota(jnp.int32, (KB, PART), 0)
                sign = (2 * (code & 1) - 1).astype(jnp.float32)
                pick = jnp.where(rows == (code >> 1), sign, 0.0).astype(jnp.bfloat16)
                dims = (((1,), (1,)), ((), ()))
                part = lax.dot_general(pick, high, dims, preferred_element_type=jnp.float32)
                part += lax.dot_general(pick, low, dims, preferred_element_type=jnp.float32)
                sketch_out[image] += part


def one_step(step, sends, finishing, todo, cotangents, projected, code, came, sketch):
    _, images, patches, _ = cotangents.shape
    block = (RW, HB)

    def fixed(i, t):
        return (0, 0)

    def whole(i, t):
        return (0, 0, 0)

    def at(i, field, t):
        return t[(step * 2 + i) * FIELDS + field]

    moving = step < sends
    piece = pl.BlockSpec(block, fixed)
    total = pl.BlockSpec(sketch.shape, whole)
    out = pl.pallas_call(
        functools.partial(step_body, step, sends, finishing),
        out_shape=[jax.ShapeDtypeStruct(block, jnp.bfloat16)] * (2 * moving)
        + [jax.ShapeDtypeStruct(sketch.shape, jnp.float32)],
        grid_spec=pltpu.PrefetchScalarGridSpec(
            num_scalar_prefetch=1,
            grid=(2,),
            in_specs=[
                pl.BlockSpec((1, 1, patches, HB), lambda i, t: (0, at(i, 0, t), 0, at(i, 1, t))),
                pl.BlockSpec((1, HB), lambda i, t: (0, at(i, 1, t))),
            ]
            + [pl.BlockSpec((1, RW, patches), lambda i, t: (at(i, 0, t), 0, 0))]
            + [piece] * len(came)
            + [total],
            out_specs=[piece] * (2 * moving) + [total],
            scratch_shapes=[pltpu.VMEM(block, jnp.float32)],
        ),
        compiler_params=pltpu.CompilerParams(vmem_limit_bytes=24 << 20),
        cost_estimate=pl.CostEstimate(
            flops=4 * RW * patches * HB,
            bytes_accessed=4 * (RW * patches + HB * patches + 2 * RW * HB),
            transcendentals=0,
        ),
    )(todo, cotangents, code, projected, *came, sketch)
    return out[:-1], out[-1]


def exchange_partials(activations, cotangents, projection, buckets, sign_bits, timesteps):
    images = activations.shape[1]
    hidden = cotangents.shape[3]
    steps = lax.axis_size("step")
    z = lax.axis_index("wide")
    core = lax.axis_index("img") % 2

    half = RW // 2
    blocks = hidden // HB
    table, sends = timetable(images * blocks, blocks)
    todo = lax.dynamic_index_in_dim(jnp.asarray(table.reshape(LINE, -1)), z, 0, keepdims=False)
    code = (2 * buckets + sign_bits).reshape(1, hidden)
    where = jnp.stack([(z - s) % LINE for s in range(LINE)] + [core, 1 - core]).astype(jnp.int32)
    mine = lax.dynamic_slice_in_dim(projection, core * half, half, 1)
    theirs = lax.dynamic_slice_in_dim(projection, (1 - core) * half, half, 1)
    pair = [(i, i ^ 1) for i in range(lax.axis_size("img"))]
    same = [
        lax.ppermute(mine, "wide", [(i, (i + s) % LINE) for i in range(LINE)])
        for s in range(1, LINE)
    ]
    same[0], theirs, todo, code, where = lax.optimization_barrier((same[0], theirs, todo, code, where))
    other = [lax.ppermute(w, "img", pair) for w in same]
    projected, whole_proj = project_first(where, activations, [mine, theirs, *same, *other])

    up = [(i, i + 1) for i in range(LINE - 1)]
    down = [(i + 1, i) for i in range(LINE - 1)]
    sketch = jnp.zeros((images, KB, RW), jnp.float32)
    came = []
    for step in range(sends + LAG):
        finishing = bool(table[:, step, :, 5].any())
        if step == AHEAD:
            later, sketch = lax.optimization_barrier((activations, sketch))
            for i in range(1, images):
                projected = project_later(i, later, whole_proj, projected)
        arrived = came[step - LAG] if step >= LAG else []
        sent, sketch = one_step(step, sends, finishing, todo, cotangents, projected, code, arrived, sketch)
        if step < sends:
            came.append([lax.ppermute(sent[0], "wide", up), lax.ppermute(sent[1], "wide", down)])

    weight = 2.0 - 1.5 * timesteps[0].astype(jnp.float32) / DIFF_STEPS
    pieces = LINE * steps
    scaled = (sketch * weight[:, None, None]).reshape(images, pieces, KB // pieces, RW)
    outgoing = jnp.swapaxes(scaled, 0, 1).reshape(pieces, images * (KB // pieces), RW)
    mixed = lax.all_to_all(outgoing, ("wide", "step"), 0, 0, tiled=True)
    return jnp.sum(mixed, axis=0).reshape(images, (KB // pieces) * RW)


def local(activations, cotangents, projection, buckets, sign_bits, timesteps):
    _, images, patches, _ = cotangents.shape
    hidden = cotangents.shape[3]
    pieces = LINE * lax.axis_size("step")
    line = (
        lax.axis_size("wide") == LINE
        and lax.axis_size("img") % 2 == 0
        and patches >= RW
        and hidden % HB == 0
        and (images * (hidden // HB)) % 2 == 0
        and hidden // HB > 2 * AHEAD
        and KB % pieces == 0
    )
    plan = exchange_partials if line else exchange_columns
    return plan(activations, cotangents, projection, buckets, sign_bits, timesteps)


def solution(mesh):
    in_specs = (
        P("step", "img", "wide", None),
        P("step", "img", "wide", None),
        P("wide", None),
        P(),
        P(),
        P("step", "img"),
    )
    out_specs = P("img", ("wide", "step"))
    return jax.shard_map(local, mesh=mesh, in_specs=in_specs, out_specs=out_specs, check_vma=False)
```

```python
import functools

import jax
import jax.numpy as jnp
import numpy as np
from jax import lax
from jax.experimental import pallas as pl
from jax.experimental.pallas import tpu as pltpu
from jax.sharding import PartitionSpec as P

RW = 512
KB = 64
DIFF_STEPS = 1000
LINE = 4
LAG = 2
HB = 512
FIELDS = 6
PART = 256
AHEAD = 2


def exchange_columns(activations, cotangents, projection, buckets, sign_bits, timesteps):
    image_count = activations.shape[1]
    projected = jnp.einsum(
        "sipd,dr->sipr",
        activations,
        lax.all_gather(projection, "wide", axis=0, tiled=True),
        preferred_element_type=jnp.float32,
    ).astype(jnp.bfloat16)
    weight = 2.0 - 1.5 * timesteps.astype(jnp.float32) / DIFF_STEPS
    sign_vals = (2 * sign_bits - 1).astype(jnp.float32)
    bucket_ids = jnp.arange(KB, dtype=jnp.int32)
    columns = lax.all_to_all(cotangents, "wide", split_axis=3, concat_axis=2, tiled=True)
    col_count = columns.shape[3]
    col_grads = jnp.einsum(
        "sipc,sipr->sicr",
        columns,
        lax.all_gather(projected, "wide", axis=2, tiled=True),
        preferred_element_type=jnp.float32,
    )
    unit = col_grads * lax.rsqrt(jnp.sum(col_grads * col_grads, axis=3, keepdims=True) + 1e-06)
    col_start = lax.axis_index("wide") * col_count
    local_buckets = lax.dynamic_slice_in_dim(buckets, col_start, col_count, 0)
    local_signs = lax.dynamic_slice_in_dim(sign_vals, col_start, col_count, 0)
    bucket_table = jnp.where(
        local_buckets[:, None] == bucket_ids[None, :], local_signs[:, None], 0.0
    )
    sketch_part = jnp.einsum("ck,sicr->sikr", bucket_table, unit, precision=lax.Precision.HIGHEST)
    scaled = sketch_part * weight[:, :, None, None]
    partial_terms = jnp.sum(scaled, axis=0).reshape(image_count, KB * RW)
    return lax.psum_scatter(partial_terms, ("wide", "step"), scatter_dimension=1, tiled=True)


def timetable(units, blocks):
    extras = 2 * LAG
    ups = (units - extras) // 2
    sends = ups + 2 * LAG
    kernels = sends + LAG
    table = np.zeros((LINE, kernels, 2, FIELDS), np.int32)

    def put(z, step, slot, unit, from_left, from_right, send):
        assert not table[z, step, slot, 4:].any()
        table[z, step, slot] = (unit // blocks, unit % blocks, from_left, from_right, send, not send)

    for u in range(ups):
        for hop in range(LINE):
            put(hop, u + hop * LAG, 0, 2 * u, hop > 0, False, hop < LINE - 1)
            put(LINE - 1 - hop, u + hop * LAG, 1, 2 * u + 1, False, hop > 0, hop < LINE - 1)
    for e in range(LAG):
        to_one, to_two = 2 * ups + e, 2 * ups + LAG + e
        early, late, last = ups + e, ups + LAG + e, ups + 2 * LAG + e
        put(0, early, 0, to_two, False, False, True)
        put(1, late, 0, to_two, True, False, True)
        put(3, late, 1, to_two, False, False, True)
        put(2, last, 1, to_two, True, True, False)
        put(3, early, 1, to_one, False, False, True)
        put(2, late, 1, to_one, False, True, True)
        put(0, late, 0, to_one, False, False, True)
        put(1, last, 0, to_one, True, True, False)
    return table, sends


def project_first_body(where, act_ref, *refs):
    (*pieces, out_ref, proj_ref, sems) = refs
    depth, half = pieces[0].shape
    count = len(pieces) // 2

    @pl.when(pl.program_id(0) == 0)
    def _():
        def each(act):
            for n, piece in enumerate(pieces):
                side, s = divmod(n, count)
                at = pl.ds(pl.multiple_of(where[2 * count + side] * half, half), half)
                rows = pl.ds(pl.multiple_of(where[s] * depth, depth), depth)

                @pl.when(where[count + s] > 0)
                def _(n=n, piece=piece, at=at, rows=rows):
                    act(pltpu.make_async_copy(piece, proj_ref.at[rows, at], sems.at[n]))

        each(lambda copy: copy.start())
        each(lambda copy: copy.wait())

    project_body(act_ref, proj_ref, out_ref)


def project_body(act_ref, proj_ref, out_ref):
    rows = jnp.dot(act_ref[0, 0], proj_ref[...], preferred_element_type=jnp.float32)
    out_ref[0] = rows.astype(jnp.bfloat16).T


def project_later_body(act_ref, proj_ref, held_ref, out_ref):
    project_body(act_ref, proj_ref, out_ref)


def project_cost(patches, width):
    return pl.CostEstimate(
        flops=2 * patches * width * RW,
        bytes_accessed=2 * (patches * (width + RW) + width * RW),
        transcendentals=0,
    )


def project_first(where, activations, pieces):
    _, images, patches, width = activations.shape
    rows = patches // 2
    part = pl.BlockSpec(memory_space=pl.ANY)
    return pl.pallas_call(
        project_first_body,
        out_shape=[
            jax.ShapeDtypeStruct((images, RW, patches), jnp.bfloat16),
            jax.ShapeDtypeStruct((width, RW), jnp.bfloat16),
        ],
        grid_spec=pltpu.PrefetchScalarGridSpec(
            num_scalar_prefetch=1,
            grid=(2,),
            in_specs=[pl.BlockSpec((1, 1, rows, width), lambda i, w: (0, 0, i, 0))]
            + [part] * len(pieces),
            out_specs=[
                pl.BlockSpec((1, RW, rows), lambda i, w: (0, 0, i)),
                pl.BlockSpec((width, RW), lambda i, w: (0, 0)),
            ],
            scratch_shapes=[pltpu.SemaphoreType.DMA((len(pieces),))],
        ),
        compiler_params=pltpu.CompilerParams(vmem_limit_bytes=44 << 20),
        cost_estimate=project_cost(patches, width),
    )(where, activations, *pieces)


def project_later(image, activations, projection, projected):
    _, images, patches, width = activations.shape
    rows = patches // 2
    return pl.pallas_call(
        project_later_body,
        out_shape=jax.ShapeDtypeStruct(projected.shape, jnp.bfloat16),
        grid=(2,),
        in_specs=[
            pl.BlockSpec((1, 1, rows, width), lambda i: (0, image, i, 0)),
            pl.BlockSpec((width, RW), lambda i: (0, 0)),
            pl.BlockSpec(memory_space=pl.ANY),
        ],
        out_specs=pl.BlockSpec((1, RW, rows), lambda i: (image, 0, i)),
        input_output_aliases={2: 0},
        compiler_params=pltpu.CompilerParams(vmem_limit_bytes=44 << 20),
        cost_estimate=project_cost(patches, width),
    )(activations, projection, projected)


def own_body(step, todo, cot_ref, proj_ref, own_ref):
    base = (step * 2 + pl.program_id(0)) * FIELDS

    @pl.when(todo[base + 4] + todo[base + 5] > 0)
    def _():
        own_ref[0] = jnp.dot(proj_ref[0], cot_ref[0, 0], preferred_element_type=jnp.float32)


def step_body(step, sends, finishing, todo, code_ref, *refs):
    refs = list(refs)
    last = step == sends + LAG - 1
    own_ref = refs.pop(0) if last else None
    cot_ref, proj_ref = (None, None) if last else (refs.pop(0), refs.pop(0))
    left_ref, right_ref = (refs.pop(0), refs.pop(0)) if step >= LAG else (None, None)
    sketch_in = refs.pop(0)
    up_ref, down_ref = (refs.pop(0), refs.pop(0)) if step < sends else (None, None)
    sketch_out, total = refs
    slot = pl.program_id(0)
    base = (step * 2 + slot) * FIELDS
    image = todo[base]
    send, finish = todo[base + 4], todo[base + 5]

    @pl.when(slot == 0)
    def _():
        sketch_out[...] = sketch_in[...]

    @pl.when(send + finish > 0)
    def _():
        if last:
            total[...] = own_ref[0]
        else:
            total[...] = jnp.dot(proj_ref[0], cot_ref[0, 0], preferred_element_type=jnp.float32)

    if left_ref is not None:
        for flag, came in ((2, left_ref), (3, right_ref)):

            @pl.when(todo[base + flag] > 0)
            def _(came=came):
                total[...] += came[...].astype(jnp.float32)

    if up_ref is not None:
        for side, out in enumerate((up_ref, down_ref)):

            @pl.when((slot == side) & (send > 0))
            def _(out=out):
                out[...] = total[...].astype(jnp.bfloat16)

    if finishing:

        @pl.when(finish > 0)
        def _():
            @pl.loop(0, HB // PART)
            def _(j):
                at = pl.ds(pl.multiple_of(j * PART, PART), PART)
                grad = total[:, at]
                scale = lax.rsqrt(jnp.sum(grad * grad, axis=0, keepdims=True) + 1e-06)
                unit = grad * scale
                high = unit.astype(jnp.bfloat16)
                low = (unit - high.astype(jnp.float32)).astype(jnp.bfloat16)
                code = code_ref[:, at]
                rows = lax.broadcasted_iota(jnp.int32, (KB, PART), 0)
                sign = (2 * (code & 1) - 1).astype(jnp.float32)
                pick = jnp.where(rows == (code >> 1), sign, 0.0).astype(jnp.bfloat16)
                dims = (((1,), (1,)), ((), ()))
                part = lax.dot_general(pick, high, dims, preferred_element_type=jnp.float32)
                part += lax.dot_general(pick, low, dims, preferred_element_type=jnp.float32)
                sketch_out[image] += part


def one_step(step, sends, finishing, todo, cotangents, projected, code, came, sketch):
    _, images, patches, _ = cotangents.shape
    block = (RW, HB)

    def fixed(i, t):
        return (0, 0)

    def whole(i, t):
        return (0, 0, 0)

    def at(i, field, t):
        return t[(step * 2 + i) * FIELDS + field]

    moving = step < sends
    piece = pl.BlockSpec(block, fixed)
    total = pl.BlockSpec(sketch.shape, whole)
    factors = [cotangents, projected]
    factor_specs = [
        pl.BlockSpec((1, 1, patches, HB), lambda i, t: (0, at(i, 0, t), 0, at(i, 1, t))),
        pl.BlockSpec((1, RW, patches), lambda i, t: (at(i, 0, t), 0, 0)),
    ]
    cost = pl.CostEstimate(
        flops=4 * RW * patches * HB,
        bytes_accessed=4 * (RW * patches + HB * patches + 2 * RW * HB),
        transcendentals=0,
    )
    params = pltpu.CompilerParams(vmem_limit_bytes=24 << 20)
    if step == sends + LAG - 1:
        own_spec = pl.BlockSpec((1, *block), lambda i, t: (i, 0, 0))
        own = pl.pallas_call(
            functools.partial(own_body, step),
            out_shape=jax.ShapeDtypeStruct((2, *block), jnp.float32),
            grid_spec=pltpu.PrefetchScalarGridSpec(
                num_scalar_prefetch=1, grid=(2,), in_specs=factor_specs, out_specs=own_spec
            ),
            compiler_params=params,
            cost_estimate=cost,
        )(todo, *factors)
        factors, factor_specs = [own], [own_spec]
    out = pl.pallas_call(
        functools.partial(step_body, step, sends, finishing),
        out_shape=[jax.ShapeDtypeStruct(block, jnp.bfloat16)] * (2 * moving)
        + [jax.ShapeDtypeStruct(sketch.shape, jnp.float32)],
        grid_spec=pltpu.PrefetchScalarGridSpec(
            num_scalar_prefetch=1,
            grid=(2,),
            in_specs=[pl.BlockSpec((1, HB), lambda i, t: (0, at(i, 1, t)))]
            + factor_specs
            + [piece] * len(came)
            + [total],
            out_specs=[piece] * (2 * moving) + [total],
            scratch_shapes=[pltpu.VMEM(block, jnp.float32)],
        ),
        compiler_params=params,
        cost_estimate=cost,
    )(todo, code, *factors, *came, sketch)
    return out[:-1], out[-1]


def exchange_partials(activations, cotangents, projection, buckets, sign_bits, timesteps):
    images = activations.shape[1]
    hidden = cotangents.shape[3]
    steps = lax.axis_size("step")
    z = lax.axis_index("wide")
    core = lax.axis_index("img") % 2

    half = RW // 2
    blocks = hidden // HB
    table, sends = timetable(images * blocks, blocks)
    todo = lax.dynamic_index_in_dim(jnp.asarray(table.reshape(LINE, -1)), z, 0, keepdims=False)
    code = (2 * buckets + sign_bits).reshape(1, hidden)
    origin = [z, (z + 2) % LINE, jnp.maximum(z - 1, 0), jnp.minimum(z + 1, LINE - 1), LINE - 1 - z]
    inner = (z > 0) & (z < LINE - 1)
    valid = [True, True, z > 0, z < LINE - 1, ~inner]
    where = jnp.stack([jnp.asarray(v, jnp.int32) for v in (*origin, *valid, core, 1 - core)])
    mine = lax.dynamic_slice_in_dim(projection, core * half, half, 1)
    theirs = lax.dynamic_slice_in_dim(projection, (1 - core) * half, half, 1)
    pair = [(i, i ^ 1) for i in range(lax.axis_size("img"))]
    up = [(i, i + 1) for i in range(LINE - 1)]
    down = [(i + 1, i) for i in range(LINE - 1)]
    second = lax.ppermute(mine, "wide", [(i, (i + 2) % LINE) for i in range(LINE)])
    nearest = [lax.ppermute(mine, "wide", up), lax.ppermute(mine, "wide", down)]
    second, theirs, todo, code, where = lax.optimization_barrier((second, theirs, todo, code, where))
    farthest = lax.ppermute(second, "wide", [(2, 3), (1, 0)])
    same = [second, *nearest, farthest]
    other = [lax.ppermute(w, "img", pair) for w in same]
    projected, whole_proj = project_first(where, activations, [mine, *same, theirs, *other])

    sketch = jnp.zeros((images, KB, RW), jnp.float32)
    came = []
    for step in range(sends + LAG):
        finishing = bool(table[:, step, :, 5].any())
        if step == AHEAD:
            later, sketch = lax.optimization_barrier((activations, sketch))
            for i in range(1, images):
                projected = project_later(i, later, whole_proj, projected)
        arrived = came[step - LAG] if step >= LAG else []
        sent, sketch = one_step(step, sends, finishing, todo, cotangents, projected, code, arrived, sketch)
        if step < sends:
            came.append([lax.ppermute(sent[0], "wide", up), lax.ppermute(sent[1], "wide", down)])

    weight = 2.0 - 1.5 * timesteps[0].astype(jnp.float32) / DIFF_STEPS
    pieces = LINE * steps
    scaled = (sketch * weight[:, None, None]).reshape(images, pieces, KB // pieces, RW)
    outgoing = jnp.swapaxes(scaled, 0, 1).reshape(pieces, images * (KB // pieces), RW)
    mixed = lax.all_to_all(outgoing, ("wide", "step"), 0, 0, tiled=True)
    return jnp.sum(mixed, axis=0).reshape(images, (KB // pieces) * RW)


def local(activations, cotangents, projection, buckets, sign_bits, timesteps):
    _, images, patches, _ = cotangents.shape
    hidden = cotangents.shape[3]
    pieces = LINE * lax.axis_size("step")
    line = (
        lax.axis_size("wide") == LINE
        and lax.axis_size("img") % 2 == 0
        and patches >= RW
        and hidden % HB == 0
        and (images * (hidden // HB)) % 2 == 0
        and hidden // HB > 2 * AHEAD
        and KB % pieces == 0
    )
    plan = exchange_partials if line else exchange_columns
    return plan(activations, cotangents, projection, buckets, sign_bits, timesteps)


def solution(mesh):
    in_specs = (
        P("step", "img", "wide", None),
        P("step", "img", "wide", None),
        P("wide", None),
        P(),
        P(),
        P("step", "img"),
    )
    out_specs = P("img", ("wide", "step"))
    return jax.shard_map(local, mesh=mesh, in_specs=in_specs, out_specs=out_specs, check_vma=False)
```
